512 devices in a mesh: dst: 128 (over z, x, core), src: 4 (over y).
Axes of the slice: x: 4, y: 4, z: 16, core: 2. Of those that a mesh axis runs over, the one named last changes fastest.
Arguments:
- query_rows: bfloat16 [131072, 512], P('dst'), may hold values from -1000 to 1000
- key_rows: bfloat16 [131072, 512], P(('dst', 'src')), may hold values from -12 to 12
- value_rows: bfloat16 [131072, 512], P(('dst', 'src')), may hold values from -6 to 6
- out_grad: bfloat16 [131072, 512], P('dst'), may hold values from -6 to 6
- node_labels: int32 [131072], replicated, may hold values from 0 to 3, as said below
- tile_list: int32 [512, 10], P(('dst', 'src')), may hold values from 0 to 19, as said below
- tile_count: int32 [512], P(('dst', 'src')), may hold values from 1 to 10
Outputs:
- query_grad: bfloat16 [131072, 512], P(('dst', 'src'))
- key_grad: bfloat16 [131072, 512], P(('dst', 'src'))
- value_grad: bfloat16 [131072, 512], P(('dst', 'src'))
The draws below stay inside these ranges and needn't reach their ends.
Inputs may be any that keep to these rules, and one draw needn't show every extreme that they name: `node_labels`: nodes 2m and 2m + 1 carry the same label. `tile_list`: row d holds distinct entries t * 5 + b with 0 <= d // 4 + b - 2 < 128; its first entry is (d % 4) * 5 + 2.
All inputs are finite; a program needn't handle non-finite values.
Results may differ from the reference program's by a relative error of at most 0.015.
Values may be sent and summed in bfloat16 or wider, within the bound.
A program may use at most 64 MiB of HBM per device.

```python
import jax
import jax.numpy as jnp
from jax import lax

HEADS = 8
HEAD_DIM = 64
WIDTH = 512
TILE = 256
REACH = 2
BAND = 5
MAXT = 10
LABELS = 4
NODES = 131072
N_DST = 128
N_SRC = 4
DEVICES = 512


def counts_law(key):
    base = jax.random.fold_in(key, 7)
    spread = jax.random.randint(jax.random.fold_in(base, 1), (DEVICES,), 0, MAXT - MAXT // 2)
    picked = jax.random.randint(jax.random.fold_in(base, 3), (), 0, 16)
    forced = jnp.arange(DEVICES) % 16 == picked
    return jnp.where(forced, MAXT, MAXT // 2 + spread).astype(jnp.int32)


def draw_tile_count(key, part):
    return counts_law(key)


def draw_tile_list(key, part):
    base = jax.random.fold_in(key, 9)
    device = jnp.arange(DEVICES)[:, None]
    position = jnp.arange(N_SRC * BAND)[None, :]
    dst_group = device // N_SRC
    quarter = device % N_SRC
    reached = dst_group + position % BAND - REACH
    usable = (reached >= 0) & (reached < N_DST)
    centre = (position // BAND == quarter) & (position % BAND == REACH)
    noise = jax.random.randint(base, (DEVICES, N_SRC * BAND), 0, 1 << 20)
    ranking = noise * 64 + position
    ranking = jnp.where(usable, ranking, ranking + (1 << 27))
    ranking = jnp.where(centre, -1, ranking)
    order = jnp.argsort(ranking, axis=1, stable=True)
    return order[:, :MAXT].astype(jnp.int32)


def draw_node_labels(key, part):
    paired = jax.random.randint(jax.random.fold_in(key, 5), (NODES // 2,), 0, LABELS)
    return jnp.repeat(paired, 2, total_repeat_length=NODES).astype(jnp.int32)


def query_key_law(key):
    base = jax.random.fold_in(key, 13)
    shape = (NODES, HEADS, HEAD_DIM)
    query_part = jnp.clip(jax.random.normal(jax.random.fold_in(base, 1), shape, jnp.float32), -6.0, 6.0)
    key_part = jnp.clip(jax.random.normal(jax.random.fold_in(base, 2), shape, jnp.float32), -6.0, 6.0)
    return (query_part.reshape(NODES, WIDTH), key_part.reshape(NODES, WIDTH))


def draw_query_rows(key, part):
    return query_key_law(key)[0].astype(jnp.bfloat16)


def draw_key_rows(key, part):
    return query_key_law(key)[1].astype(jnp.bfloat16)


def block_levels(rng, extent, pieces, smallest, largest):
    gain = 1.0
    for axis_at, blocks in pieces:
        draws = jax.random.uniform(jax.random.fold_in(jax.random.fold_in(rng, 6), axis_at), (blocks,), jnp.float32, smallest / len(pieces), largest / len(pieces))
        gain = gain * jnp.repeat(jnp.exp(draws), extent[axis_at] // blocks).reshape((-1,) + (1,) * (len(extent) - 1 - axis_at))
    return gain


def bell_draw(own_key, extent, scale, bound, cuts=(), kind=jnp.bfloat16):
    values = scale * jax.random.normal(own_key, extent, jnp.float32)
    if cuts:
        values = values * block_levels(own_key, extent, cuts, -0.22, 0.18)
    return jnp.clip(values, -bound, bound).astype(kind)


def setup_inputs(seed: int = 0) -> dict:
    arg_keys = jax.random.split(jax.random.key(seed), 8)
    query_rows = draw_query_rows(jax.random.fold_in(arg_keys[7], 71), 0)
    key_rows = draw_key_rows(jax.random.fold_in(arg_keys[7], 71), 0)
    value_rows = bell_draw(arg_keys[2], (NODES, WIDTH), 1.0, 6.0, ((0, 512),))
    out_grad = bell_draw(arg_keys[3], (NODES, WIDTH), 1.0, 6.0, ((0, 128),))
    node_labels = draw_node_labels(jax.random.fold_in(arg_keys[7], 71), 0)
    tile_list = draw_tile_list(jax.random.fold_in(arg_keys[7], 71), 0)
    tile_count = draw_tile_count(jax.random.fold_in(arg_keys[7], 71), 0)
    return {"query_rows": query_rows, "key_rows": key_rows, "value_rows": value_rows, "out_grad": out_grad, "node_labels": node_labels, "tile_list": tile_list, "tile_count": tile_count}


MASKED_SCORE = -1e30
SOFTMAX_WARMTH = 0.125


def heads_of(block):
    return block.astype(jnp.float32).reshape(block.shape[0], HEADS, HEAD_DIM)


def tile_anchor(device, position):
    dst_group = device // N_SRC
    quarter = device % N_SRC
    query_start = (dst_group * N_SRC + position // BAND) * TILE
    key_start = ((dst_group + position % BAND - REACH) * N_SRC + quarter) * TILE
    return query_start.astype(jnp.int32), key_start.astype(jnp.int32)


def over_tiles(visit, initial, tile_list, tile_count):
    def per_device(device, carried):
        def per_tile(listed, inner):
            query_start, key_start = tile_anchor(device, tile_list[device, listed])
            return visit(query_start, key_start, inner)
        return lax.fori_loop(0, tile_count[device], per_tile, carried)
    return lax.fori_loop(0, DEVICES, per_device, initial)


def probabilities(logit_scores, edge_mask, top_rows, total_rows):
    return jnp.where(edge_mask, jnp.exp(logit_scores - top_rows[:, :, None]) / total_rows[:, :, None], 0.0)


def rounded_result(values):
    return lax.optimization_barrier(values.astype(jnp.bfloat16)).astype(jnp.float32)


def reference(query_rows, key_rows, value_rows, out_grad, node_labels, tile_list, tile_count):
    def tile_scores(query_start, key_start):
        query_block_slice = heads_of(lax.dynamic_slice_in_dim(query_rows, query_start, TILE))
        key_block_slice = heads_of(lax.dynamic_slice_in_dim(key_rows, key_start, TILE))
        value_block = heads_of(lax.dynamic_slice_in_dim(value_rows, key_start, TILE))
        grad_block = heads_of(lax.dynamic_slice_in_dim(out_grad, query_start, TILE))
        logit_scores = jnp.einsum("sit,nit->isn", query_block_slice, key_block_slice) * SOFTMAX_WARMTH
        query_labels = lax.dynamic_slice_in_dim(node_labels, query_start, TILE)
        key_labels = lax.dynamic_slice_in_dim(node_labels, key_start, TILE)
        edge_mask = query_labels[:, None] == key_labels[None, :]
        logit_scores = jnp.where(edge_mask[None], logit_scores, MASKED_SCORE)
        return query_block_slice, key_block_slice, value_block, grad_block, logit_scores, edge_mask[None]

    def add_stats(query_start, key_start, carried):
        row_top, row_total = carried
        logit_scores = tile_scores(query_start, key_start)[4]
        edge_mask = tile_scores(query_start, key_start)[5]
        old_top = lax.dynamic_slice_in_dim(row_top, query_start, TILE, 1)
        old_total = lax.dynamic_slice_in_dim(row_total, query_start, TILE, 1)
        new_top = jnp.maximum(old_top, jnp.max(logit_scores, axis=2))
        weights = jnp.where(edge_mask, jnp.exp(logit_scores - new_top[:, :, None]), 0.0)
        new_total = old_total * jnp.exp(old_top - new_top) + jnp.sum(weights, axis=2)
        return (lax.dynamic_update_slice_in_dim(row_top, new_top, query_start, 1),
                lax.dynamic_update_slice_in_dim(row_total, new_total, query_start, 1))

    start_top = jnp.full((HEADS, NODES), MASKED_SCORE, jnp.float32)
    start_total = jnp.zeros((HEADS, NODES), jnp.float32)
    row_top, row_total = over_tiles(add_stats, (start_top, start_total), tile_list, tile_count)

    def add_output(query_start, key_start, attended):
        query_block_slice, key_block_slice, value_block, grad_block, logit_scores, edge_mask = tile_scores(query_start, key_start)
        top_rows = lax.dynamic_slice_in_dim(row_top, query_start, TILE, 1)
        total_rows = lax.dynamic_slice_in_dim(row_total, query_start, TILE, 1)
        probs = rounded_result(probabilities(logit_scores, edge_mask, top_rows, total_rows))
        partial_out = jnp.einsum("hqk,khd->qhd", probs, value_block).reshape(TILE, WIDTH)
        current = lax.dynamic_slice_in_dim(attended, query_start, TILE)
        return lax.dynamic_update_slice_in_dim(attended, current + partial_out, query_start, 0)

    attended = over_tiles(add_output, jnp.zeros((NODES, WIDTH), jnp.float32), tile_list, tile_count)
    delta = jnp.sum(heads_of(out_grad) * attended.reshape(NODES, HEADS, HEAD_DIM), axis=2).T

    def add_grads(query_start, key_start, carried):
        query_acc, key_acc, value_acc = carried
        query_block_slice, key_block_slice, value_block, grad_block, logit_scores, edge_mask = tile_scores(query_start, key_start)
        top_rows = lax.dynamic_slice_in_dim(row_top, query_start, TILE, 1)
        total_rows = lax.dynamic_slice_in_dim(row_total, query_start, TILE, 1)
        row_delta_terms = lax.dynamic_slice_in_dim(delta, query_start, TILE, 1)
        precise_result = probabilities(logit_scores, edge_mask, top_rows, total_rows)
        probs = rounded_result(precise_result)
        probability_gradient = jnp.einsum("sit,nit->isn", grad_block, value_block)
        score_gradient = rounded_result(precise_result * (probability_gradient - row_delta_terms[:, :, None]) * SOFTMAX_WARMTH)
        query_part = jnp.einsum("hqk,khd->qhd", score_gradient, key_block_slice).reshape(TILE, WIDTH)
        key_part = jnp.einsum("hqk,qhd->khd", score_gradient, query_block_slice).reshape(TILE, WIDTH)
        value_part = jnp.einsum("hqk,qhd->khd", probs, grad_block).reshape(TILE, WIDTH)
        query_acc = lax.dynamic_update_slice_in_dim(query_acc, lax.dynamic_slice_in_dim(query_acc, query_start, TILE) + query_part, query_start, 0)
        key_acc = lax.dynamic_update_slice_in_dim(key_acc, lax.dynamic_slice_in_dim(key_acc, key_start, TILE) + key_part, key_start, 0)
        value_acc = lax.dynamic_update_slice_in_dim(value_acc, lax.dynamic_slice_in_dim(value_acc, key_start, TILE) + value_part, key_start, 0)
        return query_acc, key_acc, value_acc

    zeros_rows = jnp.zeros((NODES, WIDTH), jnp.float32)
    query_acc, key_acc, value_acc = over_tiles(add_grads, (zeros_rows, zeros_rows, zeros_rows), tile_list, tile_count)
    return query_acc.astype(jnp.bfloat16), key_acc.astype(jnp.bfloat16), value_acc.astype(jnp.bfloat16)
```

```python
import functools
import math

import jax
import jax.numpy as jnp
from jax import lax
from jax.experimental import pallas as pl
from jax.experimental.pallas import tpu as pltpu
from jax.sharding import PartitionSpec as P

HEAD_DIM = 64
REACH = 2
BAND = 5
QUARTERS = 4
TILE = 256
LANES = 128
MASKED = -(2.0**100)
WARMTH = 0.125
TO_LOG2 = WARMTH * math.log2(math.e)
OFFSETS = (2, -2, 1, -1)
MESH = pl.DeviceIdType.MESH

NT = (((1,), (1,)), ((), ()))
NN = (((1,), (0,)), ((), ()))


def dot(a, b, dims):
    return lax.dot_general(a, b, dims, preferred_element_type=jnp.float32)


def kernel(groups, chunks, maxt, *refs):
    refs = list(refs)

    def take(n):
        got, refs[:] = refs[:n], refs[n:]
        return got

    tl, tc, q_in, k_in, v_in, g_in, lab_in = take(7)
    q_out, k_out, v_out = take(3)
    q_v, g_v = take(chunks), take(chunks)
    k_v, v_v = take(chunks), take(chunks)
    lab_q, lab_k, q_hot, k_hot, k_t = take(5)
    p_v, d_v = take(2), take(2)
    st_v = take(2)
    fin_v, dq_c, dk_c, dv_c = take(4)
    st_send, st_recv = take(2)
    kv_send, kv_recv, kv_own = take(3)
    dq_send, dq_recv, dq_own = take(3)
    inv, = take(1)
    load_sem, lab_sem, kv_ss, kv_rs, st_ss, st_rs, gr_ss, gr_rs, dq_ss, dq_rs = take(10)

    me = lax.axis_index("dst")
    quarter = lax.axis_index("src")

    def dst_peer(offset):
        return (lax.rem(me + offset + groups, groups), quarter)

    def src_peer(step):
        return (me, lax.rem(quarter + step, QUARTERS))

    lanes_of = lambda c: pl.ds(c * LANES, LANES)

    loads = []
    for c in range(chunks):
        own = []
        for n, (src, dst) in enumerate(
            (
                (k_in.at[:, lanes_of(c)], k_v[c].at[REACH]),
                (v_in.at[:, lanes_of(c)], v_v[c].at[REACH]),
                (q_in.at[:, :, lanes_of(c)], q_v[c]),
                (g_in.at[:, :, lanes_of(c)], g_v[c]),
            )
        ):
            copy = pltpu.make_async_copy(src, dst, load_sem.at[c, n])
            copy.start()
            own.append(copy)
        loads.append(own)
    lab_loads = []
    for b in range(BAND):
        group = lax.rem(me + (b - REACH) + groups, groups)
        copy = pltpu.make_async_copy(
            lab_in.at[pl.ds(group * 8, 8)], lab_k.at[b], lab_sem.at[b]
        )
        copy.start()
        lab_loads.append(copy)
    copy = pltpu.make_async_copy(lab_in.at[pl.ds(me * 8, 8)], lab_q, lab_sem.at[BAND])
    copy.start()
    lab_loads.append(copy)

    barrier = pltpu.get_barrier_semaphore()
    for offset in OFFSETS:
        pl.semaphore_signal(barrier, inc=1, device_id=dst_peer(offset), device_id_type=MESH)
    for step in range(1, QUARTERS):
        pl.semaphore_signal(barrier, inc=1, device_id=src_peer(step), device_id_type=MESH)
    pl.semaphore_wait(barrier, len(OFFSETS) + QUARTERS - 1)

    gathers = []
    for c in range(chunks):
        sent = []
        for n, offset in enumerate(OFFSETS):
            for m, (src, dst) in enumerate(((k_in, k_v[c]), (v_in, v_v[c]))):
                copy = pltpu.make_async_remote_copy(
                    src_ref=src.at[:, lanes_of(c)],
                    dst_ref=dst.at[REACH - offset],
                    send_sem=kv_ss.at[c, n, m],
                    recv_sem=kv_rs.at[c, n, m],
                    device_id=dst_peer(offset),
                    device_id_type=MESH,
                )
                copy.start()
                sent.append(copy)
        gathers.append(sent)

    count = tc[0]
    for t in range(QUARTERS):
        for b in range(BAND):
            at = jnp.int32(maxt)
            for i in range(maxt):
                hit = jnp.logical_and(tl[0, i] == t * BAND + b, i < count)
                at = jnp.where(hit, jnp.int32(i), at)
            inv[t * BAND + b] = at

    for copy in lab_loads:
        copy.wait()
    level = lax.broadcasted_iota(jnp.int32, (LANES, LANES), 0)
    for t in range(QUARTERS):
        for half in range(TILE // LANES):
            row = lab_q[pl.ds(2 * t + half, 1), :]
            hot = jnp.where(level == row, 1.0, 0.0)
            q_hot[t, pl.ds(half * LANES, LANES), :] = hot.T.astype(jnp.bfloat16)
    for b in range(BAND):
        for half in range(TILE // LANES):
            row = lab_k[b, pl.ds(2 * quarter + half, 1), :]
            hot = jnp.where(level == row, 0.0, MASKED)
            k_hot[b, pl.ds(half * LANES, LANES), :] = hot.T.astype(jnp.bfloat16)

    for ref in (dq_c, dk_c, dv_c):
        ref[maxt] = jnp.zeros(ref.shape[1:], ref.dtype)
    for ref in st_v:
        ref[maxt, pl.ds(0, 2), :] = jnp.full((2, TILE), MASKED, jnp.float32)
        ref[maxt, pl.ds(2, 6), :] = jnp.zeros((6, TILE), jnp.float32)

    first = lax.broadcasted_iota(jnp.int32, (TILE, LANES), 1) < HEAD_DIM

    def stacked(x):
        zero = jnp.zeros_like(x)
        return jnp.concatenate([jnp.where(first, x, zero), jnp.where(first, zero, x)], 0)

    def entry(i):
        code = tl[0, i]
        t = lax.div(code, jnp.int32(BAND))
        return t, code - t * BAND

    def score_pass(c):
        for copy in loads[c]:
            copy.wait()
        for copy in gathers[c]:
            copy.wait_recv()
        half = c % 2

        @pl.loop(0, BAND)
        def _(b):
            k_t[half, b] = k_v[c][b].astype(jnp.float32).T.astype(jnp.bfloat16)

        @pl.loop(0, maxt)
        def _(i):
            t, b = entry(i)
            k = stacked(k_v[c][b])
            hot = k_hot[b]
            left = jnp.concatenate([k, jnp.concatenate([hot, hot], 0)], 1)
            right = jnp.concatenate([q_v[c][t], q_hot[t]], 1)
            scores = dot(left, right, NT)
            grads = dot(stacked(v_v[c][b]), g_v[c][t], NT)
            for h in range(2):
                rows = slice(h * TILE, (h + 1) * TILE)
                s, g = scores[rows], grads[rows]
                top = jnp.max(s, axis=0, keepdims=True)
                p = jnp.exp2((s - top) * TO_LOG2)
                st_v[half][i, pl.ds(h, 1), :] = top
                st_v[half][i, pl.ds(2 + h, 1), :] = jnp.sum(p, axis=0, keepdims=True)
                st_v[half][i, pl.ds(4 + h, 1), :] = jnp.sum(p * g, axis=0, keepdims=True)
                p_v[half][i, pl.ds(h * TILE, TILE), :] = p
                d_v[half][i, pl.ds(h * TILE, TILE), :] = g

        for t in range(QUARTERS):
            at = [inv[t * BAND + b] for b in range(BAND)]
            tops = [st_v[half][a, pl.ds(0, 2), :] for a in at]
            top = functools.reduce(jnp.maximum, tops)
            total = jnp.zeros_like(top)
            delta = jnp.zeros_like(top)
            for a, one in zip(at, tops):
                scale = jnp.exp2((one - top) * TO_LOG2)
                total = total + st_v[half][a, pl.ds(2, 2), :] * scale
                delta = delta + st_v[half][a, pl.ds(4, 2), :] * scale
            for n, value in enumerate((top, total, delta)):
                st_send[c, n, pl.ds(2 * t, 2), :] = value
        sent = []
        for step in range(1, QUARTERS):
            copy = pltpu.make_async_remote_copy(
                src_ref=st_send.at[c],
                dst_ref=st_recv.at[c, step - 1],
                send_sem=st_ss.at[c, step - 1],
                recv_sem=st_rs.at[c, step - 1],
                device_id=src_peer(step),
                device_id_type=MESH,
            )
            copy.start()
            sent.append(copy)
        return sent

    def grad_pass(c, stats):
        half = c % 2
        for copy in stats:
            copy.wait_recv()
        parts = [st_send.at[c]] + [st_recv.at[c, n] for n in range(QUARTERS - 1)]
        tops = [part[0] for part in parts]
        top = functools.reduce(jnp.maximum, tops)
        total = jnp.zeros_like(top)
        delta = jnp.zeros_like(top)
        for part, one in zip(parts, tops):
            scale = jnp.exp2((one - top) * TO_LOG2)
            total = total + part[1] * scale
            delta = delta + part[2] * scale
        each = 1.0 / total
        delta = delta / total
        for t in range(QUARTERS):
            for n, value in enumerate((top, each, delta)):
                fin_v[t, pl.ds(2 * n, 2), :] = value[2 * t : 2 * t + 2]

        @pl.loop(0, maxt)
        def _(i):
            t, b = entry(i)
            probs, slopes = [], []
            for h in range(2):
                top = fin_v[t, pl.ds(h, 1), :]
                each = fin_v[t, pl.ds(2 + h, 1), :]
                delta = fin_v[t, pl.ds(4 + h, 1), :]
                own = st_v[half][i, pl.ds(h, 1), :]
                scale = jnp.exp2((own - top) * TO_LOG2) * each
                p = p_v[half][i, pl.ds(h * TILE, TILE), :] * scale
                g = d_v[half][i, pl.ds(h * TILE, TILE), :]
                probs.append(p.astype(jnp.bfloat16))
                slopes.append((p * (g - delta)).astype(jnp.bfloat16))
            dv = dot(jnp.concatenate(probs, 0), g_v[c][t], NN)
            dk = dot(jnp.concatenate(slopes, 0), q_v[c][t], NN)
            dv_c[i] = jnp.where(first, dv[:TILE], dv[TILE:])
            dk_c[i] = jnp.where(first, dk[:TILE], dk[TILE:])
            for h in range(2):
                k = k_t[half, b, pl.ds(h * HEAD_DIM, HEAD_DIM), :]
                dq_c[i, pl.ds(h * HEAD_DIM, HEAD_DIM), :] = dot(k, slopes[h], NN)

        def listed(ref, places):
            return functools.reduce(jnp.add, [ref[inv[at]] for at in places])

        sent = []
        for b in [REACH + o for o in OFFSETS] + [REACH]:
            places = [t * BAND + b for t in range(QUARTERS)]
            dk = listed(dk_c, places) * WARMTH
            dv = listed(dv_c, places)
            if b == REACH:
                kv_own[c, 0] = dk
                kv_own[c, 1] = dv
                continue
            n = OFFSETS.index(b - REACH)
            kv_send[c, n, 0] = dk.astype(jnp.bfloat16)
            kv_send[c, n, 1] = dv.astype(jnp.bfloat16)
            copy = pltpu.make_async_remote_copy(
                src_ref=kv_send.at[c, n],
                dst_ref=kv_recv.at[c, n],
                send_sem=gr_ss.at[c, n],
                recv_sem=gr_rs.at[c, n],
                device_id=dst_peer(b - REACH),
                device_id_type=MESH,
            )
            copy.start()
            sent.append(copy)
        for t in range(QUARTERS):
            dq = listed(dq_c, [t * BAND + b for b in range(BAND)]) * WARMTH
            dq_own[c, t] = dq
            dq_send[c, t] = dq.astype(jnp.bfloat16)
        for step in range(1, QUARTERS):
            copy = pltpu.make_async_remote_copy(
                src_ref=dq_send.at[c, lax.rem(quarter + step, QUARTERS)],
                dst_ref=dq_recv.at[c, step - 1],
                send_sem=dq_ss.at[c, step - 1],
                recv_sem=dq_rs.at[c, step - 1],
                device_id=src_peer(step),
                device_id_type=MESH,
            )
            copy.start()
            sent.append(copy)
        return sent

    def finish(c, sent):
        for copy in sent:
            copy.wait_recv()
        for m, out in enumerate((k_out, v_out)):
            total = kv_own[c, m]
            for n in range(len(OFFSETS)):
                total = total + kv_recv[c, n, m].astype(jnp.float32)
            out[:, lanes_of(c)] = total.astype(jnp.bfloat16)
        total = dq_own[c, quarter]
        for n in range(QUARTERS - 1):
            total = total + dq_recv[c, n].astype(jnp.float32)
        q_out[:, lanes_of(c)] = total.T.astype(jnp.bfloat16)

    stats, grads = {}, {}
    for c in range(chunks + 1):
        if c < chunks:
            stats[c] = score_pass(c)
        if c >= 1:
            grads[c - 1] = grad_pass(c - 1, stats[c - 1])
        if c >= 2:
            finish(c - 2, grads[c - 2])
    finish(chunks - 1, grads[chunks - 1])

    for sent in gathers + list(stats.values()) + list(grads.values()):
        for copy in sent:
            copy.wait_send()


def on_device(groups, query_rows, key_rows, value_rows, out_grad, node_labels, tile_list, tile_count):
    rows, width = key_rows.shape
    chunks = width // LANES
    maxt = tile_list.shape[1]
    bf16, f32 = jnp.bfloat16, jnp.float32
    vmem = pltpu.VMEM
    dma = pltpu.SemaphoreType.DMA
    near = len(OFFSETS)
    far = QUARTERS - 1
    scratch = (
        [vmem((QUARTERS, TILE, LANES), bf16)] * (2 * chunks)
        + [vmem((BAND, TILE, LANES), bf16)] * (2 * chunks)
        + [
            vmem((8, LANES), jnp.int32),
            vmem((BAND, 8, LANES), jnp.int32),
            vmem((QUARTERS, TILE, LANES), bf16),
            vmem((BAND, TILE, LANES), bf16),
            vmem((2, BAND, LANES, TILE), bf16),
        ]
        + [vmem((maxt, 2 * TILE, TILE), f32)] * 4
        + [vmem((maxt + 1, 8, TILE), f32)] * 2
        + [
            vmem((QUARTERS, 8, TILE), f32),
            vmem((maxt + 1, LANES, TILE), f32),
            vmem((maxt + 1, TILE, LANES), f32),
            vmem((maxt + 1, TILE, LANES), f32),
            vmem((chunks, 3, 8, TILE), f32),
            vmem((chunks, far, 3, 8, TILE), f32),
            vmem((chunks, near, 2, TILE, LANES), bf16),
            vmem((chunks, near, 2, TILE, LANES), bf16),
            vmem((chunks, 2, TILE, LANES), f32),
            vmem((chunks, QUARTERS, LANES, TILE), bf16),
            vmem((chunks, far, LANES, TILE), bf16),
            vmem((chunks, QUARTERS, LANES, TILE), f32),
            pltpu.SMEM((QUARTERS * BAND,), jnp.int32),
            dma((chunks, 4)),
            dma((BAND + 1,)),
            dma((chunks, near, 2)),
            dma((chunks, near, 2)),
            dma((chunks, far)),
            dma((chunks, far)),
            dma((chunks, near)),
            dma((chunks, near)),
            dma((chunks, far)),
            dma((chunks, far)),
        ]
    )
    smem = pl.BlockSpec(memory_space=pltpu.SMEM)
    anywhere = pl.BlockSpec(memory_space=pl.ANY)
    return pl.pallas_call(
        functools.partial(kernel, groups, chunks, maxt),
        out_shape=[jax.ShapeDtypeStruct((rows, width), bf16)] * 3,
        in_specs=[smem, smem] + [anywhere] * 5,
        out_specs=[pl.BlockSpec(memory_space=vmem)] * 3,
        scratch_shapes=scratch,
        compiler_params=pltpu.CompilerParams(
            collective_id=0, has_side_effects=True, vmem_limit_bytes=60 * 1024 * 1024
        ),
    )(
        tile_list,
        tile_count,
        query_rows.reshape(QUARTERS, TILE, width),
        key_rows,
        value_rows,
        out_grad.reshape(QUARTERS, TILE, width),
        node_labels.reshape(-1, LANES),
    )


def solution(mesh):
    both = P(("dst", "src"), None)
    return jax.shard_map(
        functools.partial(on_device, mesh.shape["dst"]),
        mesh=mesh,
        in_specs=(P("dst", None), both, both, P("dst", None), P(), both, P(("dst", "src"))),
        out_specs=(both, both, both),
        check_vma=False,
    )
```

```python
import functools
import math

import jax
import jax.numpy as jnp
from jax import lax
from jax.experimental import pallas as pl
from jax.experimental.pallas import tpu as pltpu
from jax.sharding import PartitionSpec as P

HEAD_DIM = 64
REACH = 2
BAND = 5
QUARTERS = 4
TILE = 256
LANES = 128
MASKED = -(2.0**100)
WARMTH = 0.125
TO_LOG2 = WARMTH * math.log2(math.e)
MESH = pl.DeviceIdType.MESH

NT = (((1,), (1,)), ((), ()))
NN = (((1,), (0,)), ((), ()))


def dot(a, b, dims):
    return lax.dot_general(a, b, dims, preferred_element_type=jnp.float32)


def kernel(groups, chunks, maxt, *refs):
    refs = list(refs)

    def take(n):
        got, refs[:] = refs[:n], refs[n:]
        return got

    tl, tc, q_in, k_in, v_in, g_in, lab_in = take(7)
    q_out, k_out, v_out = take(3)
    q_v, g_v = take(chunks), take(chunks)
    kv_v = take(chunks)
    lab_q, lab_k, q_hot, k_hot, k_t, q_t, g_t = take(7)
    p_v = take(2)
    s_v, pb_v, sb_v = take(2), take(2), take(2)
    v_t, = take(1)
    st_v = take(2)
    fin_v, dq_c, dk_c, dv_c = take(4)
    st_send, st_recv = take(2)
    kv_send, kv_recv, kv_mix, kv_own = take(4)
    dq_send, dq_recv, dq_own = take(3)
    inv, = take(1)
    own_sem, load_sem, lab_sem, kv_ss, kv_rs, st_ss, st_rs, gr_ss, gr_rs, dq_ss, dq_rs = take(11)

    me = lax.axis_index("dst")
    quarter = lax.axis_index("src")

    def dst_peer(offset):
        return (lax.rem(me + offset + groups, groups), quarter)

    def src_peer(step):
        return (me, lax.rem(quarter + step, QUARTERS))

    lanes_of = lambda c: pl.ds(c * LANES, LANES)

    side = 1 - 2 * lax.rem(me, 2)

    owns, loads = [], []
    for c in range(chunks):
        own = []
        for m, src in enumerate((k_in, v_in)):
            copy = pltpu.make_async_copy(
                src.at[:, lanes_of(c)], kv_v[c].at[REACH, m], own_sem.at[c, m]
            )
            copy.start()
            own.append(copy)
        owns.append(own)
    for c in range(chunks):
        own = []
        for n, (src, dst) in enumerate(((q_in, q_v[c]), (g_in, g_v[c]))):
            copy = pltpu.make_async_copy(src.at[:, :, lanes_of(c)], dst, load_sem.at[c, n])
            copy.start()
            own.append(copy)
        loads.append(own)
    lab_loads = []
    for b in range(BAND):
        group = lax.rem(me + (b - REACH) + groups, groups)
        copy = pltpu.make_async_copy(
            lab_in.at[pl.ds(group * 8, 8)], lab_k.at[b], lab_sem.at[b]
        )
        copy.start()
        lab_loads.append(copy)
    copy = pltpu.make_async_copy(lab_in.at[pl.ds(me * 8, 8)], lab_q, lab_sem.at[BAND])
    copy.start()
    lab_loads.append(copy)

    def remote(src, dst, send, recv, peer):
        copy = pltpu.make_async_remote_copy(
            src_ref=src,
            dst_ref=dst,
            send_sem=send,
            recv_sem=recv,
            device_id=peer,
            device_id_type=MESH,
        )
        copy.start()
        return copy

    peers = [dst_peer(2 * side), dst_peer(-2 * side), dst_peer(side)]
    peers += [src_peer(step) for step in range(1, QUARTERS)]
    barrier = pltpu.get_barrier_semaphore()
    for peer in peers:
        pl.semaphore_signal(barrier, inc=1, device_id=peer, device_id_type=MESH)
    pl.semaphore_wait(barrier, len(peers))

    gathers = []
    for c in range(chunks):
        for copy in owns[c]:
            copy.wait()
        gathers.append(
            [
                remote(
                    kv_v[c].at[REACH],
                    kv_v[c].at[REACH - offset],
                    kv_ss.at[c, n],
                    kv_rs.at[c, n],
                    dst_peer(offset),
                )
                for n, offset in enumerate((-2 * side, 2 * side, side))
            ]
        )

    def forward(c):
        gathers[c][0].wait_recv()
        gathers[c].append(
            remote(
                kv_v[c].at[REACH + 2 * side],
                kv_v[c].at[REACH + side],
                kv_ss.at[c, 3],
                kv_rs.at[c, 3],
                dst_peer(side),
            )
        )

    count = tc[0]
    for t in range(QUARTERS):
        for b in range(BAND):
            at = jnp.int32(maxt)
            for i in range(maxt):
                hit = jnp.logical_and(tl[0, i] == t * BAND + b, i < count)
                at = jnp.where(hit, jnp.int32(i), at)
            inv[t * BAND + b] = at

    for copy in lab_loads:
        copy.wait()
    level = lax.broadcasted_iota(jnp.int32, (LANES, LANES), 0)
    for t in range(QUARTERS):
        for half in range(TILE // LANES):
            row = lab_q[pl.ds(2 * t + half, 1), :]
            hot = jnp.where(level == row, 1.0, 0.0)
            q_hot[t, pl.ds(half * LANES, LANES), :] = hot.T.astype(jnp.bfloat16)
    for b in range(BAND):
        for half in range(TILE // LANES):
            row = lab_k[b, pl.ds(2 * quarter + half, 1), :]
            hot = jnp.where(level == row, 0.0, MASKED)
            k_hot[b, pl.ds(half * LANES, LANES), :] = hot.T.astype(jnp.bfloat16)

    for ref in (dq_c, dk_c, dv_c):
        ref[maxt] = jnp.zeros(ref.shape[1:], ref.dtype)
    for ref in st_v:
        ref[maxt, pl.ds(0, 2), :] = jnp.full((2, TILE), MASKED, jnp.float32)
        ref[maxt, pl.ds(2, 6), :] = jnp.zeros((6, TILE), jnp.float32)

    first = lax.broadcasted_iota(jnp.int32, (TILE, LANES), 1) < HEAD_DIM

    ones = jnp.ones((16, TILE), jnp.bfloat16)

    def stacked(x):
        zero = jnp.zeros_like(x)
        return jnp.concatenate([jnp.where(first, x, zero), jnp.where(first, zero, x)], 0)

    def joined(ref, h):
        rows = pl.ds(h * TILE, TILE)
        return jnp.concatenate([ref[n, rows, :] for n in range(TILE // LANES)], 1)

    def entry(i):
        code = tl[0, i]
        t = lax.div(code, jnp.int32(BAND))
        return t, code - t * BAND

    def score_pass(c):
        for copy in gathers[c][1:]:
            copy.wait_recv()
        half = c % 2

        @pl.loop(0, BAND)
        def _(b):
            k_t[half, b] = kv_v[c][b, 0].T
            v_t[b] = kv_v[c][b, 1].T

        def products(i, odd):
            t, b = entry(i)
            hot = k_hot[b]
            left = jnp.concatenate(
                [stacked(kv_v[c][b, 0]), jnp.concatenate([hot, hot], 0)], 1
            )
            right = jnp.concatenate([q_v[c][t], q_hot[t]], 1)
            s_v[odd][...] = dot(left, right, NT)

        def weigh(i, odd):
            for h in range(2):
                rows = pl.ds(h * TILE, TILE)
                for n in range(TILE // LANES):
                    lanes = pl.ds(n * LANES, LANES)
                    s = s_v[odd][rows, lanes]
                    top = jnp.max(s, axis=0, keepdims=True)
                    p = jnp.exp2((s - top) * TO_LOG2)
                    p_v[half][i, rows, lanes] = p
                    pb_v[odd][n, rows, :] = p.astype(jnp.bfloat16)
                    st_v[half][i, pl.ds(h, 1), lanes] = top

        def attend(i, odd):
            t, b = entry(i)
            for h in range(2):
                lanes = pl.ds(h * HEAD_DIM, HEAD_DIM)
                left = jnp.concatenate([v_t[b, lanes, :], ones], 0)
                out = dot(left, joined(pb_v[odd], h), NN)
                delta = out[:HEAD_DIM] * g_t[c, t, lanes, :].astype(jnp.float32)
                st_v[half][i, pl.ds(2 + h, 1), :] = out[HEAD_DIM : HEAD_DIM + 1]
                st_v[half][i, pl.ds(4 + h, 1), :] = jnp.sum(delta, axis=0, keepdims=True)

        def visit(n):
            products(2 * n + 1, 1)
            weigh(2 * n, 0)
            attend(jnp.maximum(2 * n - 1, 0), 1)
            products(jnp.minimum(2 * n + 2, maxt - 1), 0)
            weigh(2 * n + 1, 1)
            attend(2 * n, 0)

        pairs = maxt // 2
        products(0, 0)
        pl.loop(0, pairs // 2)(visit)
        if c + 1 < chunks:
            forward(c + 1)
        pl.loop(pairs // 2, pairs)(visit)
        attend(maxt - 1, 1)

        for t in range(QUARTERS):
            at = [inv[t * BAND + b] for b in range(BAND)]
            tops = [st_v[half][a, pl.ds(0, 2), :] for a in at]
            top = functools.reduce(jnp.maximum, tops)
            total = jnp.zeros_like(top)
            delta = jnp.zeros_like(top)
            for a, one in zip(at, tops):
                scale = jnp.exp2((one - top) * TO_LOG2)
                total = total + st_v[half][a, pl.ds(2, 2), :] * scale
                delta = delta + st_v[half][a, pl.ds(4, 2), :] * scale
            for n, value in enumerate((top, total, delta)):
                st_send[c, n, pl.ds(2 * t, 2), :] = value
        sent = []
        for step in range(1, QUARTERS):
            copy = pltpu.make_async_remote_copy(
                src_ref=st_send.at[c],
                dst_ref=st_recv.at[c, step - 1],
                send_sem=st_ss.at[c, step - 1],
                recv_sem=st_rs.at[c, step - 1],
                device_id=src_peer(step),
                device_id_type=MESH,
            )
            copy.start()
            sent.append(copy)
        return sent

    def grad_pass(c, stats):
        half = c % 2
        for copy in stats:
            copy.wait_recv()
        parts = [st_send.at[c]] + [st_recv.at[c, n] for n in range(QUARTERS - 1)]
        tops = [part[0] for part in parts]
        top = functools.reduce(jnp.maximum, tops)
        total = jnp.zeros_like(top)
        delta = jnp.zeros_like(top)
        for part, one in zip(parts, tops):
            scale = jnp.exp2((one - top) * TO_LOG2)
            total = total + part[1] * scale
            delta = delta + part[2] * scale
        each = 1.0 / total
        delta = delta / total
        for t in range(QUARTERS):
            for n, value in enumerate((top, each, delta)):
                fin_v[t, pl.ds(2 * n, 2), :] = value[2 * t : 2 * t + 2]

        def prob_grads(i, odd):
            t, b = entry(i)
            s_v[odd][...] = dot(stacked(kv_v[c][b, 1]), g_v[c][t], NT)

        def slopes(i, odd):
            t, _ = entry(i)
            for h in range(2):
                rows = pl.ds(h * TILE, TILE)
                for n in range(TILE // LANES):
                    lanes = pl.ds(n * LANES, LANES)
                    top = fin_v[t, pl.ds(h, 1), lanes]
                    each = fin_v[t, pl.ds(2 + h, 1), lanes]
                    delta = fin_v[t, pl.ds(4 + h, 1), lanes]
                    own = st_v[half][i, pl.ds(h, 1), lanes]
                    scale = jnp.exp2((own - top) * TO_LOG2) * each
                    p = p_v[half][i, rows, lanes] * scale
                    pb_v[odd][n, rows, :] = p.astype(jnp.bfloat16)
                    sb_v[odd][n, rows, :] = (p * (s_v[odd][rows, lanes] - delta)).astype(
                        jnp.bfloat16
                    )

        def gradients(i, odd):
            t, b = entry(i)
            for h in range(2):
                lanes = pl.ds(h * HEAD_DIM, HEAD_DIM)
                slope = joined(sb_v[odd], h)
                dv_c[i, lanes, :] = dot(g_t[c, t, lanes, :], joined(pb_v[odd], h), NT)
                dk_c[i, lanes, :] = dot(q_t[c, t, lanes, :], slope, NT)
                dq_c[i, lanes, :] = dot(k_t[half, b, lanes, :], slope, NN)

        prob_grads(0, 0)
        prob_grads(1, 1)
        slopes(0, 0)

        @pl.loop(0, maxt // 2)
        def _(n):
            after = jnp.minimum(2 * n + 2, maxt - 2)
            slopes(2 * n + 1, 1)
            prob_grads(after, 0)
            gradients(2 * n, 0)
            slopes(after, 0)
            prob_grads(after + 1, 1)
            gradients(2 * n + 1, 1)

        def listed(ref, places):
            return functools.reduce(jnp.add, [ref[inv[at]] for at in places])

        def band_sum(b):
            places = [t * BAND + b for t in range(QUARTERS)]
            return listed(dk_c, places) * WARMTH, listed(dv_c, places)

        sent = []
        for n, (b, dst, peer) in enumerate(
            (
                (REACH - side, kv_mix.at[c], side),
                (REACH - 2 * side, kv_recv.at[c, 0], -2 * side),
                (REACH + side, kv_recv.at[c, 1], side),
            )
        ):
            for m, value in enumerate(band_sum(b)):
                kv_send[c, n, m] = value.astype(jnp.bfloat16)
            sent.append(
                remote(kv_send.at[c, n], dst, gr_ss.at[c, n], gr_rs.at[c, n], dst_peer(peer))
            )
        for m, value in enumerate(band_sum(REACH)):
            kv_own[c, 0, m] = value
        for m, value in enumerate(band_sum(REACH + 2 * side)):
            kv_own[c, 1, m] = value
        for t in range(QUARTERS):
            dq = listed(dq_c, [t * BAND + b for b in range(BAND)]) * WARMTH
            dq_own[c, t] = dq
            dq_send[c, t] = dq.astype(jnp.bfloat16)
        for step in range(1, QUARTERS):
            copy = pltpu.make_async_remote_copy(
                src_ref=dq_send.at[c, lax.rem(quarter + step, QUARTERS)],
                dst_ref=dq_recv.at[c, step - 1],
                send_sem=dq_ss.at[c, step - 1],
                recv_sem=dq_rs.at[c, step - 1],
                device_id=src_peer(step),
                device_id_type=MESH,
            )
            copy.start()
            sent.append(copy)
        return sent

    def merge(c, sent):
        sent[0].wait_recv()
        for m in range(2):
            mixed = kv_own[c, 1, m] + kv_mix[c, m].astype(jnp.float32)
            kv_send[c, 3, m] = mixed.astype(jnp.bfloat16)
        sent.append(
            remote(
                kv_send.at[c, 3], kv_recv.at[c, 2], gr_ss.at[c, 3], gr_rs.at[c, 3], dst_peer(2 * side)
            )
        )

    def finish(c, sent):
        for copy in sent[1:]:
            copy.wait_recv()
        for m, out in enumerate((k_out, v_out)):
            total = kv_own[c, 0, m]
            for n in range(3):
                total = total + kv_recv[c, n, m].astype(jnp.float32)
            out[:, lanes_of(c)] = total.T.astype(jnp.bfloat16)
        total = dq_own[c, quarter]
        for n in range(QUARTERS - 1):
            total = total + dq_recv[c, n].astype(jnp.float32)
        q_out[:, lanes_of(c)] = total.T.astype(jnp.bfloat16)

    stats, grads = {}, {}
    for c in range(chunks):
        for copy in loads[c]:
            copy.wait()

        @pl.loop(0, QUARTERS)
        def _(t):
            q_t[c, t] = q_v[c][t].T
            g_t[c, t] = g_v[c][t].T

    forward(0)
    for c in range(chunks + 1):
        if c < chunks:
            stats[c] = score_pass(c)
        if c >= 2:
            merge(c - 2, grads[c - 2])
        if c >= 1:
            grads[c - 1] = grad_pass(c - 1, stats[c - 1])
        if c >= 3:
            finish(c - 3, grads[c - 3])
    finish(chunks - 2, grads[chunks - 2])
    merge(chunks - 1, grads[chunks - 1])
    finish(chunks - 1, grads[chunks - 1])

    for sent in gathers + list(stats.values()) + list(grads.values()):
        for copy in sent:
            copy.wait_send()


def handed_on(*refs):
    for src, dst in zip(refs[:3], refs[3:]):
        dst[...] = src[...]


def on_device(groups, query_rows, key_rows, value_rows, out_grad, node_labels, tile_list, tile_count):
    rows, width = key_rows.shape
    chunks = width // LANES
    maxt = tile_list.shape[1]
    bf16, f32 = jnp.bfloat16, jnp.float32
    vmem = pltpu.VMEM
    dma = pltpu.SemaphoreType.DMA
    near = 4
    far = QUARTERS - 1
    scratch = (
        [vmem((QUARTERS, TILE, LANES), bf16)] * (2 * chunks)
        + [vmem((BAND, 2, TILE, LANES), bf16)] * chunks
        + [
            vmem((8, LANES), jnp.int32),
            vmem((BAND, 8, LANES), jnp.int32),
            vmem((QUARTERS, TILE, LANES), bf16),
            vmem((BAND, TILE, LANES), bf16),
            vmem((2, BAND, LANES, TILE), bf16),
            vmem((chunks, QUARTERS, LANES, TILE), bf16),
            vmem((chunks, QUARTERS, LANES, TILE), bf16),
        ]
        + [vmem((maxt, 2 * TILE, TILE), f32)] * 2
        + [vmem((2 * TILE, TILE), f32)] * 2
        + [vmem((TILE // LANES, 2 * TILE, LANES), bf16)] * 4
        + [vmem((BAND, LANES, TILE), bf16)]
        + [vmem((maxt + 1, 8, TILE), f32)] * 2
        + [
            vmem((QUARTERS, 8, TILE), f32),
            vmem((maxt + 1, LANES, TILE), f32),
            vmem((maxt + 1, LANES, TILE), f32),
            vmem((maxt + 1, LANES, TILE), f32),
            vmem((chunks, 3, 8, TILE), f32),
            vmem((chunks, far, 3, 8, TILE), f32),
            vmem((chunks, near, 2, LANES, TILE), bf16),
            vmem((chunks, 3, 2, LANES, TILE), bf16),
            vmem((chunks, 2, LANES, TILE), bf16),
            vmem((chunks, 2, 2, LANES, TILE), f32),
            vmem((chunks, QUARTERS, LANES, TILE), bf16),
            vmem((chunks, far, LANES, TILE), bf16),
            vmem((chunks, QUARTERS, LANES, TILE), f32),
            pltpu.SMEM((QUARTERS * BAND,), jnp.int32),
            dma((chunks, 2)),
            dma((chunks, 2)),
            dma((BAND + 1,)),
            dma((chunks, near)),
            dma((chunks, near)),
            dma((chunks, far)),
            dma((chunks, far)),
            dma((chunks, near)),
            dma((chunks, near)),
            dma((chunks, far)),
            dma((chunks, far)),
        ]
    )
    smem = pl.BlockSpec(memory_space=pltpu.SMEM)
    anywhere = pl.BlockSpec(memory_space=pl.ANY)
    results = pl.pallas_call(
        functools.partial(kernel, groups, chunks, maxt),
        out_shape=[jax.ShapeDtypeStruct((rows, width), bf16)] * 3,
        in_specs=[smem, smem] + [anywhere] * 5,
        out_specs=[pl.BlockSpec(memory_space=vmem)] * 3,
        scratch_shapes=scratch,
        compiler_params=pltpu.CompilerParams(
            collective_id=0, has_side_effects=True, vmem_limit_bytes=44 * 1024 * 1024
        ),
    )(
        tile_list,
        tile_count,
        pltpu.with_memory_space_constraint(query_rows.reshape(QUARTERS, TILE, width), pltpu.HBM),
        pltpu.with_memory_space_constraint(key_rows, pltpu.HBM),
        pltpu.with_memory_space_constraint(value_rows, pltpu.HBM),
        pltpu.with_memory_space_constraint(out_grad.reshape(QUARTERS, TILE, width), pltpu.HBM),
        pltpu.with_memory_space_constraint(node_labels.reshape(-1, LANES), pltpu.HBM),
    )
    whole = [pl.BlockSpec(memory_space=vmem)] * 3
    return pl.pallas_call(
        handed_on,
        out_shape=[jax.ShapeDtypeStruct((rows, width), bf16)] * 3,
        in_specs=whole,
        out_specs=whole,
        compiler_params=pltpu.CompilerParams(vmem_limit_bytes=4 * 1024 * 1024),
    )(*results)


def solution(mesh):
    both = P(("dst", "src"), None)
    return jax.shard_map(
        functools.partial(on_device, mesh.shape["dst"]),
        mesh=mesh,
        in_specs=(P("dst", None), both, both, P("dst", None), P(), both, P(("dst", "src"))),
        out_specs=(both, both, both),
        check_vma=False,
    )
```

```python
import functools
import math

import jax
import jax.numpy as jnp
from jax import lax
from jax.experimental import pallas as pl
from jax.experimental.pallas import tpu as pltpu
from jax.sharding import PartitionSpec as P

HEAD_DIM = 64
REACH = 2
BAND = 5
QUARTERS = 4
TILE = 256
LANES = 128
MASKED = -(2.0**100)
WARMTH = 0.125
TO_LOG2 = WARMTH * math.log2(math.e)
MESH = pl.DeviceIdType.MESH

NT = (((1,), (1,)), ((), ()))
NN = (((1,), (0,)), ((), ()))


def dot(a, b, dims):
    return lax.dot_general(a, b, dims, preferred_element_type=jnp.float32)


def kernel(groups, chunks, maxt, *refs):
    refs = list(refs)

    def take(n):
        got, refs[:] = refs[:n], refs[n:]
        return got

    tl, tc, q_in, k_in, v_in, g_in, lab_in = take(7)
    q_out, k_out, v_out = take(3)
    q_v, g_v = take(chunks), take(chunks)
    kv_v = take(chunks)
    lab_q, lab_k, q_hot, k_hot, k_t, q_t, g_t = take(7)
    p_v = take(2)
    s_v, pb_v, sb_v = take(2), take(2), take(2)
    v_t, = take(1)
    st_v = take(2)
    fin_v, dq_c, dk_c, dv_c = take(4)
    st_send, st_recv = take(2)
    kv_send, kv_recv, kv_mix, kv_own = take(4)
    dq_send, dq_recv, dq_own = take(3)
    inv, = take(1)
    own_sem, load_sem, lab_sem, kv_ss, kv_rs, st_ss, st_rs, gr_ss, gr_rs, dq_ss, dq_rs = take(11)

    me = lax.axis_index("dst")
    quarter = lax.axis_index("src")

    def dst_peer(offset):
        return (lax.rem(me + offset + groups, groups), quarter)

    def src_peer(step):
        return (me, lax.rem(quarter + step, QUARTERS))

    lanes_of = lambda c: pl.ds(c * LANES, LANES)

    side = 1 - 2 * lax.rem(me, 2)

    owns, loads = [], []
    for c in range(chunks):
        own = []
        for m, src in enumerate((k_in, v_in)):
            copy = pltpu.make_async_copy(
                src.at[:, lanes_of(c)], kv_v[c].at[REACH, m], own_sem.at[c, m]
            )
            copy.start()
            own.append(copy)
        owns.append(own)
    for c in range(chunks):
        own = []
        for n, (src, dst) in enumerate(((q_in, q_v[c]), (g_in, g_v[c]))):
            copy = pltpu.make_async_copy(src.at[:, :, lanes_of(c)], dst, load_sem.at[c, n])
            copy.start()
            own.append(copy)
        loads.append(own)
    lab_loads = []
    for b in range(BAND):
        group = lax.rem(me + (b - REACH) + groups, groups)
        copy = pltpu.make_async_copy(
            lab_in.at[pl.ds(group * 8, 8)], lab_k.at[b], lab_sem.at[b]
        )
        copy.start()
        lab_loads.append(copy)
    copy = pltpu.make_async_copy(lab_in.at[pl.ds(me * 8, 8)], lab_q, lab_sem.at[BAND])
    copy.start()
    lab_loads.append(copy)

    def remote(src, dst, send, recv, peer):
        copy = pltpu.make_async_remote_copy(
            src_ref=src,
            dst_ref=dst,
            send_sem=send,
            recv_sem=recv,
            device_id=peer,
            device_id_type=MESH,
        )
        copy.start()
        return copy

    peers = [dst_peer(2 * side), dst_peer(-2 * side), dst_peer(side)]
    peers += [src_peer(step) for step in range(1, QUARTERS)]
    barrier = pltpu.get_barrier_semaphore()
    for peer in peers:
        pl.semaphore_signal(barrier, inc=1, device_id=peer, device_id_type=MESH)
    pl.semaphore_wait(barrier, len(peers))

    gathers = []
    for c in range(chunks):
        for copy in owns[c]:
            copy.wait()
        gathers.append(
            [
                remote(
                    kv_v[c].at[REACH],
                    kv_v[c].at[REACH - offset],
                    kv_ss.at[c, n],
                    kv_rs.at[c, n],
                    dst_peer(offset),
                )
                for n, offset in enumerate((-2 * side, 2 * side, side))
            ]
        )

    def forward(c):
        gathers[c][0].wait_recv()
        gathers[c].append(
            remote(
                kv_v[c].at[REACH + 2 * side],
                kv_v[c].at[REACH + side],
                kv_ss.at[c, 3],
                kv_rs.at[c, 3],
                dst_peer(side),
            )
        )

    count = tc[0]
    for t in range(QUARTERS):
        for b in range(BAND):
            at = jnp.int32(maxt)
            for i in range(maxt):
                hit = jnp.logical_and(tl[0, i] == t * BAND + b, i < count)
                at = jnp.where(hit, jnp.int32(i), at)
            inv[t * BAND + b] = at

    for copy in lab_loads:
        copy.wait()
    level = lax.broadcasted_iota(jnp.int32, (LANES, LANES), 0)
    for t in range(QUARTERS):
        for half in range(TILE // LANES):
            row = lab_q[pl.ds(2 * t + half, 1), :]
            hot = jnp.where(level == row, 1.0, 0.0)
            q_hot[t, pl.ds(half * LANES, LANES), :] = hot.T.astype(jnp.bfloat16)
    for b in range(BAND):
        for half in range(TILE // LANES):
            row = lab_k[b, pl.ds(2 * quarter + half, 1), :]
            hot = jnp.where(level == row, 0.0, MASKED)
            k_hot[b, pl.ds(half * LANES, LANES), :] = hot.T.astype(jnp.bfloat16)

    for ref in (dq_c, dk_c, dv_c):
        ref[maxt] = jnp.zeros(ref.shape[1:], ref.dtype)
    for ref in st_v:
        ref[maxt, pl.ds(0, 2), :] = jnp.full((2, TILE), MASKED, jnp.float32)
        ref[maxt, pl.ds(2, 6), :] = jnp.zeros((6, TILE), jnp.float32)

    first = lax.broadcasted_iota(jnp.int32, (TILE, LANES), 1) < HEAD_DIM

    ones = jnp.ones((16, TILE), jnp.bfloat16)

    def stacked(x):
        zero = jnp.zeros_like(x)
        return jnp.concatenate([jnp.where(first, x, zero), jnp.where(first, zero, x)], 0)

    def joined(ref, h):
        rows = pl.ds(h * TILE, TILE)
        return jnp.concatenate([ref[n, rows, :] for n in range(TILE // LANES)], 1)

    def entry(i):
        code = tl[0, i]
        t = lax.div(code, jnp.int32(BAND))
        return t, code - t * BAND

    def arrive(c):
        for copy in gathers[c][1:]:
            copy.wait_recv()

    def score_pass(c):
        half = c % 2
        if c < 2:
            arrive(c)

        if c < 2:

            @pl.loop(0, BAND)
            def _(b):
                v_t[half, b] = kv_v[c][b, 1].T

        def products(i, odd):
            t, b = entry(i)
            hot = k_hot[b]
            left = jnp.concatenate(
                [stacked(kv_v[c][b, 0]), jnp.concatenate([hot, hot], 0)], 1
            )
            right = jnp.concatenate([q_v[c][t], q_hot[t]], 1)
            s_v[odd][...] = dot(left, right, NT)

        def weigh(i, odd):
            for h in range(2):
                rows = pl.ds(h * TILE, TILE)
                for n in range(TILE // LANES):
                    lanes = pl.ds(n * LANES, LANES)
                    s = s_v[odd][rows, lanes]
                    top = jnp.max(s, axis=0, keepdims=True)
                    p = jnp.exp2((s - top) * TO_LOG2)
                    p_v[half][i, rows, lanes] = p
                    pb_v[odd][n, rows, :] = p.astype(jnp.bfloat16)
                    st_v[half][i, pl.ds(h, 1), lanes] = top

        def attend(i, odd):
            t, b = entry(i)
            for h in range(2):
                lanes = pl.ds(h * HEAD_DIM, HEAD_DIM)
                left = jnp.concatenate([v_t[half, b, lanes, :], ones], 0)
                out = dot(left, joined(pb_v[odd], h), NN)
                delta = out[:HEAD_DIM] * g_t[c, t, lanes, :].astype(jnp.float32)
                st_v[half][i, pl.ds(2 + h, 1), :] = out[HEAD_DIM : HEAD_DIM + 1]
                st_v[half][i, pl.ds(4 + h, 1), :] = jnp.sum(delta, axis=0, keepdims=True)

        def visit(n):
            k_t[half, n] = kv_v[c][n, 0].T
            products(2 * n + 1, 1)
            weigh(2 * n, 0)
            attend(jnp.maximum(2 * n - 1, 0), 1)
            products(jnp.minimum(2 * n + 2, maxt - 1), 0)
            weigh(2 * n + 1, 1)
            attend(2 * n, 0)

        pairs = maxt // 2
        products(0, 0)
        pl.loop(0, pairs // 2)(visit)
        if c + 1 < chunks:
            forward(c + 1)
        pl.loop(pairs // 2, pairs)(visit)
        attend(maxt - 1, 1)

        for t in range(QUARTERS):
            at = [inv[t * BAND + b] for b in range(BAND)]
            tops = [st_v[half][a, pl.ds(0, 2), :] for a in at]
            top = functools.reduce(jnp.maximum, tops)
            total = jnp.zeros_like(top)
            delta = jnp.zeros_like(top)
            for a, one in zip(at, tops):
                scale = jnp.exp2((one - top) * TO_LOG2)
                total = total + st_v[half][a, pl.ds(2, 2), :] * scale
                delta = delta + st_v[half][a, pl.ds(4, 2), :] * scale
            for n, value in enumerate((top, total, delta)):
                st_send[c, n, pl.ds(2 * t, 2), :] = value
        sent = []
        for step in range(1, QUARTERS):
            copy = pltpu.make_async_remote_copy(
                src_ref=st_send.at[c],
                dst_ref=st_recv.at[c, step - 1],
                send_sem=st_ss.at[c, step - 1],
                recv_sem=st_rs.at[c, step - 1],
                device_id=src_peer(step),
                device_id_type=MESH,
            )
            copy.start()
            sent.append(copy)
        return sent

    def grad_pass(c, stats):
        half = c % 2
        for copy in stats:
            copy.wait_recv()
        parts = [st_send.at[c]] + [st_recv.at[c, n] for n in range(QUARTERS - 1)]
        tops = [part[0] for part in parts]
        top = functools.reduce(jnp.maximum, tops)
        total = jnp.zeros_like(top)
        delta = jnp.zeros_like(top)
        for part, one in zip(parts, tops):
            scale = jnp.exp2((one - top) * TO_LOG2)
            total = total + part[1] * scale
            delta = delta + part[2] * scale
        each = 1.0 / total
        delta = delta / total
        for t in range(QUARTERS):
            for n, value in enumerate((top, each, delta)):
                fin_v[t, pl.ds(2 * n, 2), :] = value[2 * t : 2 * t + 2]

        def prob_grads(i, odd):
            t, b = entry(i)
            s_v[odd][...] = dot(stacked(kv_v[c][b, 1]), g_v[c][t], NT)

        def slopes(i, odd):
            t, _ = entry(i)
            for h in range(2):
                rows = pl.ds(h * TILE, TILE)
                for n in range(TILE // LANES):
                    lanes = pl.ds(n * LANES, LANES)
                    top = fin_v[t, pl.ds(h, 1), lanes]
                    each = fin_v[t, pl.ds(2 + h, 1), lanes]
                    delta = fin_v[t, pl.ds(4 + h, 1), lanes]
                    own = st_v[half][i, pl.ds(h, 1), lanes]
                    scale = jnp.exp2((own - top) * TO_LOG2) * each
                    p = p_v[half][i, rows, lanes] * scale
                    pb_v[odd][n, rows, :] = p.astype(jnp.bfloat16)
                    sb_v[odd][n, rows, :] = (p * (s_v[odd][rows, lanes] - delta)).astype(
                        jnp.bfloat16
                    )

        def gradients(i, odd):
            t, b = entry(i)
            for h in range(2):
                lanes = pl.ds(h * HEAD_DIM, HEAD_DIM)
                slope = joined(sb_v[odd], h)
                dv_c[i, lanes, :] = dot(g_t[c, t, lanes, :], joined(pb_v[odd], h), NT)
                dk_c[i, lanes, :] = dot(q_t[c, t, lanes, :], slope, NT)
                dq_c[i, lanes, :] = dot(k_t[half, b, lanes, :], slope, NN)

        nearing = 2 <= c + 2 < chunks
        if nearing:
            arrive(c + 2)
        prob_grads(0, 0)
        prob_grads(1, 1)
        slopes(0, 0)

        @pl.loop(0, maxt // 2)
        def _(n):
            after = jnp.minimum(2 * n + 2, maxt - 2)
            if nearing:
                v_t[half, n] = kv_v[c + 2][n, 1].T
            slopes(2 * n + 1, 1)
            prob_grads(after, 0)
            gradients(2 * n, 0)
            slopes(after, 0)
            prob_grads(after + 1, 1)
            gradients(2 * n + 1, 1)

        def listed(ref, places):
            return functools.reduce(jnp.add, [ref[inv[at]] for at in places])

        def band_sum(b):
            places = [t * BAND + b for t in range(QUARTERS)]
            return listed(dk_c, places) * WARMTH, listed(dv_c, places)

        sent = []
        for n, (b, dst, peer) in enumerate(
            (
                (REACH - side, kv_mix.at[c], side),
                (REACH - 2 * side, kv_recv.at[c, 0], -2 * side),
                (REACH + side, kv_recv.at[c, 1], side),
            )
        ):
            for m, value in enumerate(band_sum(b)):
                kv_send[c, n, m] = value.astype(jnp.bfloat16)
            sent.append(
                remote(kv_send.at[c, n], dst, gr_ss.at[c, n], gr_rs.at[c, n], dst_peer(peer))
            )
        for m, value in enumerate(band_sum(REACH)):
            kv_own[c, 0, m] = value
        for m, value in enumerate(band_sum(REACH + 2 * side)):
            kv_own[c, 1, m] = value
        for t in range(QUARTERS):
            dq = listed(dq_c, [t * BAND + b for b in range(BAND)]) * WARMTH
            dq_own[c, t] = dq
            dq_send[c, t] = dq.astype(jnp.bfloat16)
        for step in range(1, QUARTERS):
            copy = pltpu.make_async_remote_copy(
                src_ref=dq_send.at[c, lax.rem(quarter + step, QUARTERS)],
                dst_ref=dq_recv.at[c, step - 1],
                send_sem=dq_ss.at[c, step - 1],
                recv_sem=dq_rs.at[c, step - 1],
                device_id=src_peer(step),
                device_id_type=MESH,
            )
            copy.start()
            sent.append(copy)
        return sent

    def merge(c, sent):
        sent[0].wait_recv()
        for m in range(2):
            mixed = kv_own[c, 1, m] + kv_mix[c, m].astype(jnp.float32)
            kv_send[c, 3, m] = mixed.astype(jnp.bfloat16)
        sent.append(
            remote(
                kv_send.at[c, 3], kv_recv.at[c, 2], gr_ss.at[c, 3], gr_rs.at[c, 3], dst_peer(2 * side)
            )
        )

    def finish(c, sent):
        for copy in sent[1:]:
            copy.wait_recv()
        for m, out in enumerate((k_out, v_out)):
            total = kv_own[c, 0, m]
            for n in range(3):
                total = total + kv_recv[c, n, m].astype(jnp.float32)
            out[:, lanes_of(c)] = total.T.astype(jnp.bfloat16)
        total = dq_own[c, quarter]
        for n in range(QUARTERS - 1):
            total = total + dq_recv[c, n].astype(jnp.float32)
        q_out[:, lanes_of(c)] = total.T.astype(jnp.bfloat16)

    stats, grads = {}, {}
    def turn(c):
        for copy in loads[c]:
            copy.wait()

        @pl.loop(0, QUARTERS)
        def _(t):
            q_t[c, t] = q_v[c][t].T
            g_t[c, t] = g_v[c][t].T

    early = chunks // 2
    for c in range(early):
        turn(c)
    forward(0)
    for c in range(early, chunks):
        turn(c)
    for c in range(chunks + 1):
        if c < chunks:
            stats[c] = score_pass(c)
        if c >= 2:
            merge(c - 2, grads[c - 2])
        if c >= 1:
            grads[c - 1] = grad_pass(c - 1, stats[c - 1])
        if c >= 3:
            finish(c - 3, grads[c - 3])
    finish(chunks - 2, grads[chunks - 2])
    merge(chunks - 1, grads[chunks - 1])
    finish(chunks - 1, grads[chunks - 1])

    for sent in gathers + list(stats.values()) + list(grads.values()):
        for copy in sent:
            copy.wait_send()


def handed_on(*refs):
    for src, dst in zip(refs[:3], refs[3:]):
        dst[...] = src[...]


def on_device(groups, query_rows, key_rows, value_rows, out_grad, node_labels, tile_list, tile_count):
    rows, width = key_rows.shape
    chunks = width // LANES
    maxt = tile_list.shape[1]
    bf16, f32 = jnp.bfloat16, jnp.float32
    vmem = pltpu.VMEM
    dma = pltpu.SemaphoreType.DMA
    near = 4
    far = QUARTERS - 1
    scratch = (
        [vmem((QUARTERS, TILE, LANES), bf16)] * (2 * chunks)
        + [vmem((BAND, 2, TILE, LANES), bf16)] * chunks
        + [
            vmem((8, LANES), jnp.int32),
            vmem((BAND, 8, LANES), jnp.int32),
            vmem((QUARTERS, TILE, LANES), bf16),
            vmem((BAND, TILE, LANES), bf16),
            vmem((2, BAND, LANES, TILE), bf16),
            vmem((chunks, QUARTERS, LANES, TILE), bf16),
            vmem((chunks, QUARTERS, LANES, TILE), bf16),
        ]
        + [vmem((maxt, 2 * TILE, TILE), f32)] * 2
        + [vmem((2 * TILE, TILE), f32)] * 2
        + [vmem((TILE // LANES, 2 * TILE, LANES), bf16)] * 4
        + [vmem((2, BAND, LANES, TILE), bf16)]
        + [vmem((maxt + 1, 8, TILE), f32)] * 2
        + [
            vmem((QUARTERS, 8, TILE), f32),
            vmem((maxt + 1, LANES, TILE), f32),
            vmem((maxt + 1, LANES, TILE), f32),
            vmem((maxt + 1, LANES, TILE), f32),
            vmem((chunks, 3, 8, TILE), f32),
            vmem((chunks, far, 3, 8, TILE), f32),
            vmem((chunks, near, 2, LANES, TILE), bf16),
            vmem((chunks, 3, 2, LANES, TILE), bf16),
            vmem((chunks, 2, LANES, TILE), bf16),
            vmem((chunks, 2, 2, LANES, TILE), f32),
            vmem((chunks, QUARTERS, LANES, TILE), bf16),
            vmem((chunks, far, LANES, TILE), bf16),
            vmem((chunks, QUARTERS, LANES, TILE), f32),
            pltpu.SMEM((QUARTERS * BAND,), jnp.int32),
            dma((chunks, 2)),
            dma((chunks, 2)),
            dma((BAND + 1,)),
            dma((chunks, near)),
            dma((chunks, near)),
            dma((chunks, far)),
            dma((chunks, far)),
            dma((chunks, near)),
            dma((chunks, near)),
            dma((chunks, far)),
            dma((chunks, far)),
        ]
    )
    smem = pl.BlockSpec(memory_space=pltpu.SMEM)
    anywhere = pl.BlockSpec(memory_space=pl.ANY)
    results = pl.pallas_call(
        functools.partial(kernel, groups, chunks, maxt),
        out_shape=[jax.ShapeDtypeStruct((rows, width), bf16)] * 3,
        in_specs=[smem, smem] + [anywhere] * 5,
        out_specs=[pl.BlockSpec(memory_space=vmem)] * 3,
        scratch_shapes=scratch,
        compiler_params=pltpu.CompilerParams(
            collective_id=0, has_side_effects=True, vmem_limit_bytes=44 * 1024 * 1024
        ),
    )(
        tile_list,
        tile_count,
        pltpu.with_memory_space_constraint(query_rows.reshape(QUARTERS, TILE, width), pltpu.HBM),
        pltpu.with_memory_space_constraint(key_rows, pltpu.HBM),
        pltpu.with_memory_space_constraint(value_rows, pltpu.HBM),
        pltpu.with_memory_space_constraint(out_grad.reshape(QUARTERS, TILE, width), pltpu.HBM),
        pltpu.with_memory_space_constraint(node_labels.reshape(-1, LANES), pltpu.HBM),
    )
    whole = [pl.BlockSpec(memory_space=vmem)] * 3
    return pl.pallas_call(
        handed_on,
        out_shape=[jax.ShapeDtypeStruct((rows, width), bf16)] * 3,
        in_specs=whole,
        out_specs=whole,
        compiler_params=pltpu.CompilerParams(vmem_limit_bytes=4 * 1024 * 1024),
    )(*results)


def solution(mesh):
    both = P(("dst", "src"), None)
    return jax.shard_map(
        functools.partial(on_device, mesh.shape["dst"]),
        mesh=mesh,
        in_specs=(P("dst", None), both, both, P("dst", None), P(), both, P(("dst", "src"))),
        out_specs=(both, both, both),
        check_vma=False,
    )
```
